32 devices in a mesh: tm: 2 (over x), east: 4 (over y, core), north: 4 (over z).
Axes of the slice: x: 2, y: 2, z: 4, core: 2. Of those that a mesh axis runs over, the one named last changes fastest.
Arguments:
- agents: bfloat16 [2, 8, 8, 128, 256], P('tm', 'east', 'north'), may hold values from -12 to 12
- query_weight: bfloat16 [256, 256], replicated, may hold values from -1 to 1
- key_weight: bfloat16 [256, 256], replicated, may hold values from -1 to 1
- value_weight: bfloat16 [256, 256], replicated, may hold values from -0.375 to 0.375
- out_weight: bfloat16 [256, 256], replicated, may hold values from -0.375 to 0.375
- grad_output: bfloat16 [2, 8, 8, 128, 256], P('tm', 'east', 'north'), may hold values from -6 to 6
- same_lists: int32 [2, 8, 8, 6], P('tm', 'east', 'north'), may hold values from -1 to 127, as said below
- prev_lists: int32 [2, 8, 8, 3], P('tm', 'east', 'north'), may hold values from -1 to 63, as said below
- counts: int32 [2, 8, 8], P('tm', 'east', 'north'), may hold values from 1 to 128
Outputs:
- attn_output: bfloat16 [2, 8, 8, 128, 256], P('tm', 'east', 'north')
- agent_grad: bfloat16 [2, 8, 8, 128, 256], P('tm', 'east', 'north')
- query_weight_grad: float32 [256, 256], replicated
- key_weight_grad: float32 [256, 256], replicated
- value_weight_grad: float32 [256, 256], replicated
- out_weight_grad: float32 [256, 256], replicated
The draws below stay inside these ranges and needn't reach their ends.
Inputs may be any that keep to these rules, and one draw needn't show every extreme that they name: `same_lists`: each row starts with the query block's own id; the others are distinct ids of blocks of the same timestep at most one block away along each grid dimension; -1 marks an empty entry and occurs only where fewer than 6 such blocks lie inside the grid. `prev_lists`: at timestep 1 each row starts with the id of the block at the same position at timestep 0, followed by distinct ids of timestep-0 blocks at most one block away along each grid dimension; every entry at timestep 0 is -1.
All inputs are finite; a program needn't handle non-finite values.
Results may differ from the reference program's by a relative error of at most 0.012.
Values may be sent and summed in bfloat16 or wider, within the bound.
A program may use at most 128 MiB of HBM per device.

```python
import math
import jax
import jax.numpy as jnp
from jax import lax

D = 256
HEADS = 4
HD = 64
BLK = 128
K_SAME = 6
K_PREV = 3
STEPS = 2
GE = 8
GN = 8


def draw_agents(key, part):
    shape = (STEPS, GE, GN, BLK // 2, 2, D)
    result = jnp.clip(jax.random.normal(jax.random.fold_in(key, 1), shape, jnp.float32), -6.0, 6.0)
    return result.reshape(STEPS, GE, GN, BLK, D).astype(jnp.bfloat16)


def common_matrix(key):
    return jnp.clip(jax.random.normal(jax.random.fold_in(key, 11), (D, D), jnp.float32), -6.0, 6.0)


def draw_query_weight(key, part):
    return (common_matrix(key) / jnp.sqrt(jnp.float32(D))).astype(jnp.bfloat16)


def draw_key_weight(key, part):
    fresh = jnp.clip(jax.random.normal(jax.random.fold_in(key, 12), (D, D), jnp.float32), -6.0, 6.0)
    result = fresh
    return (result / jnp.sqrt(jnp.float32(D))).astype(jnp.bfloat16)


def neighbour_lists(key, keep_count, step_back):
    offsets = jnp.arange(9, dtype=jnp.int32)
    east_step = offsets // 3 - 1
    north_step = offsets % 3 - 1
    east_grid = jnp.arange(GE, dtype=jnp.int32)[:, None, None] + east_step[None, None, :]
    north_grid = jnp.arange(GN, dtype=jnp.int32)[None, :, None] + north_step[None, None, :]
    inside = (east_grid >= 0) & (east_grid < GE) & (north_grid >= 0) & (north_grid < GN)
    ranks = jax.random.randint(key, (STEPS, GE, GN, 9), 0, 4096, dtype=jnp.int32) * 16 + offsets
    ranks = jnp.where(offsets == 4, jnp.int32(1 << 20), ranks)
    ranks = jnp.where(inside[None], ranks, jnp.int32(-1))
    picked, chosen = lax.top_k(ranks, keep_count)
    east_full = jnp.broadcast_to(east_grid[None], (STEPS, GE, GN, 9))
    north_full = jnp.broadcast_to(north_grid[None], (STEPS, GE, GN, 9))
    east_pick = jnp.take_along_axis(east_full, chosen, axis=-1)
    north_pick = jnp.take_along_axis(north_full, chosen, axis=-1)
    step_index = jnp.arange(STEPS, dtype=jnp.int32)[:, None, None, None] - step_back
    block_ids = (step_index * GE + east_pick) * GN + north_pick
    usable = (picked >= 0) & (step_index >= 0)
    return jnp.where(usable, block_ids, jnp.int32(-1)).astype(jnp.int32)


def draw_same_lists(key, part):
    return neighbour_lists(jax.random.fold_in(key, 21), K_SAME, 0)


def draw_prev_lists(key, part):
    return neighbour_lists(jax.random.fold_in(key, 22), K_PREV, 1)


def plant(drawn, own_key, least, largest):
    shape = drawn.shape
    index_at = [jax.random.randint(jax.random.fold_in(own_key, axis), (), 0, shape[axis]) for axis in range(len(shape))]
    drawn = drawn.at[tuple(index_at)].set(least)
    longest = shape.index(max(shape))
    index_at[longest] = (index_at[longest] + 1) % shape[longest]
    return drawn.at[tuple(index_at)].set(largest)


def block_scale(stream_key, extent, split, smallest, high):
    level, own = 1.0, jax.random.fold_in(stream_key, 6)
    for position, shards_of in split:
        draws = jnp.exp(jax.random.uniform(jax.random.fold_in(own, position), (shards_of,), jnp.float32, smallest / len(split), high / len(split)))
        level = level * jnp.repeat(draws, extent[position] // shards_of).reshape([-1 if axis == position else 1 for axis in range(len(extent))])
    return level


def noise(stream_key, extent, scale, reach, pieces=(), kind=jnp.bfloat16):
    values = jax.random.normal(stream_key, extent, jnp.float32) * scale
    if len(pieces) > 0:
        values = block_scale(stream_key, extent, pieces, -0.22, 0.18) * values
    return jnp.clip(values, min=-reach, max=reach).astype(kind)


def setup_inputs(seed: int = 0) -> dict:
    streams_of = jax.random.split(jax.random.key(seed), 10)
    agents = draw_agents(jax.random.fold_in(streams_of[9], 71), 0)
    query_weight = draw_query_weight(jax.random.fold_in(streams_of[9], 71), 0)
    key_weight = draw_key_weight(jax.random.fold_in(streams_of[9], 71), 0)
    value_weight = noise(streams_of[3], (D, D), D ** -0.5, 0.375)
    out_weight = noise(streams_of[4], (D, D), D ** -0.5, 0.375)
    grad_output = noise(streams_of[5], (STEPS, GE, GN, BLK, D), 1.0, 6.0, ((0, 2), (1, 4), (2, 4)))
    same_lists = draw_same_lists(jax.random.fold_in(streams_of[9], 71), 0)
    prev_lists = draw_prev_lists(jax.random.fold_in(streams_of[9], 71), 0)
    counts = plant(jax.random.randint(streams_of[8], (STEPS, GE, GN), 1, BLK + 1), jax.random.fold_in(streams_of[8], 1), 1, BLK).astype(jnp.int32)
    return {"agents": agents, "query_weight": query_weight, "key_weight": key_weight, "value_weight": value_weight, "out_weight": out_weight, "grad_output": grad_output, "same_lists": same_lists, "prev_lists": prev_lists, "counts": counts}


NEG_FILL = -1e+30

def attend_block(query_block, grad_block, key_set, value_set, key_ok):
    block_rows = query_block.shape[0]
    query_heads = query_block.astype(jnp.float32).reshape(block_rows, HEADS, HD)
    grad_heads = grad_block.astype(jnp.float32).reshape(block_rows, HEADS, HD)
    key_heads = key_set.astype(jnp.float32).reshape(-1, HEADS, HD)
    value_heads = value_set.astype(jnp.float32).reshape(-1, HEADS, HD)
    score_scale = 1.0 / math.sqrt(HD)
    scores = jnp.einsum('qhd,khd->hqk', query_heads, key_heads) * score_scale
    scores = jnp.where(key_ok[None, None, :], scores, NEG_FILL)
    row_max = lax.optimization_barrier(jnp.max(scores, axis=-1, keepdims=True))
    raised = jnp.exp(scores - row_max)
    soft_prob = raised / lax.optimization_barrier(jnp.sum(raised, axis=-1, keepdims=True))
    prob_half = soft_prob.astype(jnp.bfloat16)
    prob_wide = prob_half.astype(jnp.float32)
    attended = jnp.einsum('hqk,khd->qhd', prob_wide, value_heads).astype(jnp.bfloat16).reshape(block_rows, D)
    grad_prob = jnp.einsum('qhd,khd->hqk', grad_heads, value_heads)
    row_delta = lax.optimization_barrier(jnp.sum(soft_prob * grad_prob, axis=-1, keepdims=True))
    grad_score = (soft_prob * (grad_prob - row_delta) * score_scale).astype(jnp.bfloat16).astype(jnp.float32)
    grad_query = jnp.einsum('hqk,khd->qhd', grad_score, key_heads).reshape(block_rows, D)
    grad_key = jnp.einsum('hqk,qhd->khd', grad_score, query_heads).reshape(-1, D)
    grad_value = jnp.einsum('hqk,qhd->khd', prob_wide, grad_heads).reshape(-1, D)
    return (attended, grad_query, jnp.concatenate([grad_key, grad_value], axis=-1))

def reference(agents, query_weight, key_weight, value_weight, out_weight, grad_output, same_lists, prev_lists, counts):
    block_total = STEPS * GE * GN
    list_len = K_SAME + K_PREV
    agent_rows = agents.reshape(block_total * BLK, D)
    query_rows = jnp.dot(agent_rows, query_weight, preferred_element_type=jnp.float32).astype(jnp.bfloat16)
    key_rows = jnp.dot(agent_rows, key_weight, preferred_element_type=jnp.float32).astype(jnp.bfloat16)
    value_rows = jnp.dot(agent_rows, value_weight, preferred_element_type=jnp.float32).astype(jnp.bfloat16)
    query_blocks = query_rows.reshape(block_total, BLK, D)
    key_blocks = key_rows.reshape(block_total, BLK, D)
    value_blocks = value_rows.reshape(block_total, BLK, D)
    flat_counts = counts.reshape(block_total)
    row_index = jnp.arange(BLK, dtype=jnp.int32)
    row_valid = row_index[None, :] < flat_counts[:, None]
    out_rows = grad_output.reshape(block_total * BLK, D)
    grad_attn = jnp.dot(out_rows, out_weight.T, preferred_element_type=jnp.float32)
    grad_attn = jnp.where(row_valid.reshape(-1, 1), grad_attn, 0.0).astype(jnp.bfloat16).reshape(block_total, BLK, D)
    entries = jnp.concatenate([same_lists.reshape(block_total, K_SAME), prev_lists.reshape(block_total, K_PREV)], axis=1)

    def one_block(query_block, grad_block, entry_row):
        listed = entry_row >= 0
        safe_ids = jnp.where(listed, entry_row, 0).astype(jnp.int32)
        key_ok = listed[:, None] & (row_index[None, :] < flat_counts[safe_ids][:, None])
        key_set = key_blocks[safe_ids].reshape(list_len * BLK, D)
        value_set = value_blocks[safe_ids].reshape(list_len * BLK, D)
        return attend_block(query_block, grad_block, key_set, value_set, key_ok.reshape(-1))

    def group_step(grad_table, group):
        query_group, grad_group, entry_group = group
        attended, grad_query, grad_pairs = jax.vmap(one_block)(query_group, grad_group, entry_group)
        safe_group = jnp.where(entry_group >= 0, entry_group, 0).astype(jnp.int32).reshape(-1)
        grad_table = grad_table.at[safe_group].add(grad_pairs.reshape(-1, BLK, 2 * D))
        return (grad_table, (attended, grad_query))
    group_count = STEPS * GE
    start_table = jnp.zeros((block_total, BLK, 2 * D), jnp.float32)
    grad_table, (attended, grad_query) = lax.scan(group_step, start_table, (query_blocks.reshape(group_count, GN, BLK, D), grad_attn.reshape(group_count, GN, BLK, D), entries.reshape(group_count, GN, list_len)))
    attended = attended.reshape(block_total, BLK, D)
    attended = jnp.where(row_valid[:, :, None], attended, jnp.zeros_like(attended))
    attended_rows = attended.reshape(-1, D)
    attn_output = jnp.dot(attended_rows, out_weight, preferred_element_type=jnp.float32).astype(jnp.bfloat16).reshape(agents.shape)
    grad_query_half = grad_query.reshape(-1, D).astype(jnp.bfloat16)
    grad_key_half = grad_table[:, :, :D].reshape(-1, D).astype(jnp.bfloat16)
    grad_value_half = grad_table[:, :, D:].reshape(-1, D).astype(jnp.bfloat16)
    agent_grad = jnp.dot(grad_query_half, query_weight.T, preferred_element_type=jnp.float32) + jnp.dot(grad_key_half, key_weight.T, preferred_element_type=jnp.float32) + jnp.dot(grad_value_half, value_weight.T, preferred_element_type=jnp.float32)
    agent_grad = agent_grad.astype(jnp.bfloat16).reshape(agents.shape)
    norm_factor = 1.0 / math.sqrt(block_total * BLK)
    query_weight_grad = jnp.dot(agent_rows.T, grad_query_half, preferred_element_type=jnp.float32) * norm_factor
    key_weight_grad = jnp.dot(agent_rows.T, grad_key_half, preferred_element_type=jnp.float32) * norm_factor
    value_weight_grad = jnp.dot(agent_rows.T, grad_value_half, preferred_element_type=jnp.float32) * norm_factor
    out_weight_grad = jnp.dot(attended_rows.T, out_rows, preferred_element_type=jnp.float32) * norm_factor
    return (attn_output, agent_grad, query_weight_grad, key_weight_grad, value_weight_grad, out_weight_grad)
```

```python
import math

import jax
import jax.numpy as jnp
from jax import lax
from jax.experimental import pallas as pl
from jax.experimental.pallas import tpu as pltpu
from jax.sharding import PartitionSpec as P

HEADS = 4
NEG_FILL = -1e30
MARK = 64.0
EMPTY_ABOVE = 32.0


def shifted(x, axis, by):
    peers = lax.axis_size(axis)
    pairs = [(i, i + by) for i in range(peers) if 0 <= i + by < peers]
    return lax.ppermute(x, axis, pairs)


def padded(cells, axis, dim):
    head = lax.slice_in_dim(cells, 0, 1, axis=dim)
    tail = lax.slice_in_dim(cells, cells.shape[dim] - 1, cells.shape[dim], axis=dim)
    return jnp.concatenate([shifted(tail, axis, 1), cells, shifted(head, axis, -1)], axis=dim)


def dot(left, right, left_dim, right_dim):
    return lax.dot_general(
        left, right, (((left_dim,), (right_dim,)), ((), ())), preferred_element_type=jnp.float32
    )


def layer_kernel(
    own_slots,
    list_len,
    entry_ref,
    count_ref,
    table_ref,
    agent_ref,
    out_grad_ref,
    wq_ref,
    wkv_ref,
    wo_ref,
    attn_ref,
    part_ref,
    own_ref,
    query_term_ref,
    pair_term_ref,
    out_term_ref,
    kv_ref,
    acc_ref,
    kset_ref,
    vset_ref,
    bias_ref,
    score_ref,
    gprob_ref,
    prob_ref,
    gscore_ref,
    qbd_ref,
    gbd_ref,
):
    slots, rows, width = table_ref.shape
    blocks = agent_ref.shape[0]
    head_size = width // HEADS
    scale = 1.0 / math.sqrt(head_size)
    bf16 = jnp.bfloat16

    def project(i, c):
        at = pl.ds(i * 4, 4)
        kv = dot(table_ref[at].reshape(4 * rows, width), wkv_ref[...], 1, 0)
        kv_ref[at] = kv.astype(bf16).reshape(4, rows, 2 * width)
        acc_ref[at] = jnp.zeros((4, rows, 2 * width), jnp.float32)
        return c

    lax.fori_loop(0, slots // 4, project, 0)
    query_term_ref[...] = jnp.zeros_like(query_term_ref)
    pair_term_ref[...] = jnp.zeros_like(pair_term_ref)
    out_term_ref[...] = jnp.zeros_like(out_term_ref)
    lane = lax.broadcasted_iota(jnp.int32, (rows, width), 1)
    row = lax.broadcasted_iota(jnp.int32, (rows, width), 0)
    step = 3 * rows
    chunks = [pl.ds(i * step, step) for i in range(list_len // 3)]

    def diagonal(full):
        parts = [
            full[h * head_size : (h + 1) * head_size, h * rows : (h + 1) * rows]
            for h in range(HEADS)
        ]
        return jnp.concatenate(parts, axis=0).T

    def block(b, c):
        a = agent_ref[b]
        og = out_grad_ref[b]
        ok = row < count_ref[b]
        q = dot(a, wq_ref[...], 1, 0).astype(bf16).astype(jnp.float32) * scale
        g = jnp.where(ok, dot(og, wo_ref[...], 1, 1), 0.0)
        for h in range(HEADS):
            mine = (lane >= h * head_size) & (lane < (h + 1) * head_size)
            qbd_ref[pl.ds(h * rows, rows)] = jnp.where(mine, q, 0.0).astype(bf16)
            gbd_ref[pl.ds(h * rows, rows)] = jnp.where(mine, g, 0.0).astype(bf16)
        for e in range(list_len):
            entry = entry_ref[b * list_len + e]
            slot = jnp.maximum(entry, 0)
            at = pl.ds(e * rows, rows)
            kset_ref[at] = kv_ref[slot, :, :width]
            vset_ref[at] = kv_ref[slot, :, width:]
            mark = table_ref[slot, :, :128].astype(jnp.float32)
            gone = jnp.where(mark > EMPTY_ABOVE, NEG_FILL, 0.0)
            gone = jnp.where(entry < 0, NEG_FILL, gone)
            bias_ref[at] = jnp.broadcast_to(gone[:, :1], (rows, 128))
        top = jnp.full((1, HEADS * rows), 2 * NEG_FILL, jnp.float32)
        for at in chunks:
            s = dot(kset_ref[at], qbd_ref[...], 1, 1)
            s = s + jnp.concatenate([bias_ref[at]] * (HEADS * rows // 128), axis=1)
            score_ref[at] = s
            top = jnp.maximum(top, jnp.max(s, axis=0, keepdims=True))
            gprob_ref[at] = dot(vset_ref[at], gbd_ref[...], 1, 1)
        total = jnp.zeros_like(top)
        delta = jnp.zeros_like(top)
        for at in chunks:
            e = jnp.exp(score_ref[at] - top)
            score_ref[at] = e
            total = total + jnp.sum(e, axis=0, keepdims=True)
            delta = delta + jnp.sum(e * gprob_ref[at], axis=0, keepdims=True)
        inv = 1.0 / total
        delta = delta * inv
        for at in chunks:
            p = score_ref[at] * inv
            prob_ref[at] = p.astype(bf16)
            gscore_ref[at] = (p * (gprob_ref[at] - delta)).astype(bf16)
        for i, at in enumerate(chunks):
            gk = dot(gscore_ref[at], qbd_ref[...], 1, 0)
            gv = dot(prob_ref[at], gbd_ref[...], 1, 0)
            for j in range(3):
                slot = jnp.maximum(entry_ref[b * list_len + i * 3 + j], 0)
                acc_ref[slot, :, :width] += gk[j * rows : (j + 1) * rows]
                acc_ref[slot, :, width:] += gv[j * rows : (j + 1) * rows]
        att = diagonal(dot(vset_ref[...], prob_ref[...], 0, 0))
        gq = diagonal(dot(kset_ref[...], gscore_ref[...], 0, 0)) * scale
        att = jnp.where(ok, att, 0.0).astype(bf16)
        gq = gq.astype(bf16)
        attn_ref[b] = dot(att, wo_ref[...], 1, 0).astype(bf16)
        out_term_ref[...] += dot(att, og, 0, 0)
        query_term_ref[...] += dot(a, gq, 0, 0)
        own_ref[b] = dot(gq, wq_ref[...], 1, 1)
        return c

    lax.fori_loop(0, blocks, block, 0)

    def finish(i, c):
        at = pl.ds(i * 4, 4)
        pair = acc_ref[at].astype(bf16).reshape(4 * rows, 2 * width)
        pair_term_ref[...] += dot(table_ref[at].reshape(4 * rows, width), pair, 0, 0)
        part = dot(pair, wkv_ref[...], 1, 1)
        part_ref[at] = part.astype(bf16).reshape(4, rows, width)
        return c

    lax.fori_loop(0, slots // 4, finish, 0)
    for b, slot in enumerate(own_slots):
        pair = acc_ref[slot].astype(bf16)
        own_ref[b] += dot(pair, wkv_ref[...], 1, 1)


def per_device(
    agents,
    query_weight,
    key_weight,
    value_weight,
    out_weight,
    grad_output,
    same_lists,
    prev_lists,
    counts,
):
    _, east_blocks, north_blocks, rows, width = agents.shape
    own_blocks = east_blocks * north_blocks
    same_count = same_lists.shape[-1]
    list_len = same_count + prev_lists.shape[-1]
    span_east = east_blocks + 2
    span_north = north_blocks + 2
    rim = span_east * span_north
    row_index = jnp.arange(rows, dtype=jnp.int32)
    valid = row_index < counts[..., None]
    marked = jnp.where(valid[..., None], agents, jnp.asarray(MARK, agents.dtype))
    cells = jnp.concatenate([marked, shifted(marked, "tm", 1)], axis=0)
    cells = padded(padded(cells, "east", 1), "north", 2)
    table = cells.reshape(2 * rim, rows, width)
    grid_east = east_blocks * lax.axis_size("east")
    grid_north = north_blocks * lax.axis_size("north")
    first_east = lax.axis_index("east") * east_blocks
    first_north = lax.axis_index("north") * north_blocks

    def local_slot(ids, base):
        place = ids % (grid_east * grid_north)
        east_pos = place // grid_north - first_east + 1
        north_pos = place % grid_north - first_north + 1
        return jnp.where(ids >= 0, base + east_pos * span_north + north_pos, -1)

    entries = jnp.concatenate(
        [
            local_slot(same_lists.reshape(own_blocks, same_count), 0),
            local_slot(prev_lists.reshape(own_blocks, list_len - same_count), rim),
        ],
        axis=1,
    ).reshape(-1)
    own_slots = [
        (e + 1) * span_north + n + 1 for e in range(east_blocks) for n in range(north_blocks)
    ]
    keys = list_len * rows
    lanes = HEADS * rows
    f32, bf16 = jnp.float32, jnp.bfloat16
    vmem = pl.BlockSpec(memory_space=pltpu.VMEM)
    smem = pl.BlockSpec(memory_space=pltpu.SMEM)
    attn, part, own, query_term, pair_term, out_term = pl.pallas_call(
        lambda *refs: layer_kernel(own_slots, list_len, *refs),
        out_shape=(
            jax.ShapeDtypeStruct((own_blocks, rows, width), bf16),
            jax.ShapeDtypeStruct((2 * rim, rows, width), bf16),
            jax.ShapeDtypeStruct((own_blocks, rows, width), f32),
            jax.ShapeDtypeStruct((width, width), f32),
            jax.ShapeDtypeStruct((width, 2 * width), f32),
            jax.ShapeDtypeStruct((width, width), f32),
        ),
        in_specs=[smem, smem] + [vmem] * 6,
        out_specs=[vmem] * 6,
        scratch_shapes=[
            pltpu.VMEM((2 * rim, rows, 2 * width), bf16),
            pltpu.VMEM((2 * rim, rows, 2 * width), f32),
            pltpu.VMEM((keys, width), bf16),
            pltpu.VMEM((keys, width), bf16),
            pltpu.VMEM((keys, 128), f32),
            pltpu.VMEM((keys, lanes), f32),
            pltpu.VMEM((keys, lanes), f32),
            pltpu.VMEM((keys, lanes), bf16),
            pltpu.VMEM((keys, lanes), bf16),
            pltpu.VMEM((lanes, width), bf16),
            pltpu.VMEM((lanes, width), bf16),
        ],
        compiler_params=pltpu.CompilerParams(vmem_limit_bytes=56 * 1024 * 1024),
    )(
        entries,
        counts.reshape(-1),
        table,
        agents.reshape(own_blocks, rows, width),
        grad_output.reshape(own_blocks, rows, width),
        query_weight,
        jnp.concatenate([key_weight, value_weight], axis=1),
        out_weight,
    )
    part = part.reshape(2, span_east, span_north, rows, width)
    upper = shifted(part[:, :, -1], "north", 1)
    lower = shifted(part[:, :, 0], "north", -1)
    def edge(cells, at):
        col = cells[:, at].astype(f32)
        col = col.at[:, 0].add(upper[:, at].astype(f32))
        return col.at[:, -1].add(lower[:, at].astype(f32))

    inner = part[:, :, 1:-1]
    east_upper = shifted(edge(inner, span_east - 1).astype(bf16), "east", 1)
    east_lower = shifted(edge(inner, 0).astype(bf16), "east", -1)
    own_cells = own.reshape(1, east_blocks, north_blocks, rows, width)
    core = jnp.concatenate([own_cells, inner[1:, 1:-1].astype(f32)], axis=0)
    core = core.at[:, :, 0].add(upper[:, 1:-1].astype(f32))
    core = core.at[:, :, -1].add(lower[:, 1:-1].astype(f32))
    core = core.at[:, 0].add(east_upper.astype(f32))
    core = core.at[:, -1].add(east_lower.astype(f32))
    agent_grad = core[:1] + shifted(core[1:].astype(bf16), "tm", -1).astype(f32)
    agent_grad = agent_grad.astype(bf16)
    query_sum, pair_sum, out_sum = lax.psum(
        (query_term, pair_term, out_term), ("tm", "east", "north")
    )
    total_rows = (
        lax.axis_size("tm")
        * lax.axis_size("east")
        * lax.axis_size("north")
        * own_blocks
        * rows
    )
    norm = 1.0 / math.sqrt(total_rows)
    return (
        attn.reshape(agents.shape),
        agent_grad,
        query_sum * norm,
        pair_sum[:, :width] * norm,
        pair_sum[:, width:] * norm,
        out_sum * norm,
    )


def solution(mesh):
    cells = P("tm", "east", "north", None, None)
    lists = P("tm", "east", "north", None)
    in_specs = (cells, P(), P(), P(), P(), cells, lists, lists, P("tm", "east", "north"))
    out_specs = (cells, cells, P(), P(), P(), P())
    return jax.shard_map(
        per_device, mesh=mesh, in_specs=in_specs, out_specs=out_specs, check_vma=False
    )
```

```python
import math

import jax
import jax.numpy as jnp
from jax import lax
from jax.experimental import pallas as pl
from jax.experimental.pallas import tpu as pltpu
from jax.sharding import PartitionSpec as P

HEADS = 4
NEG_FILL = -1e30
MARK = 64.0
EMPTY_ABOVE = 32.0


def shifted(x, axis, by):
    peers = lax.axis_size(axis)
    pairs = [(i, i + by) for i in range(peers) if 0 <= i + by < peers]
    return lax.ppermute(x, axis, pairs)


def padded(cells, axis, dim):
    head = lax.slice_in_dim(cells, 0, 1, axis=dim)
    tail = lax.slice_in_dim(cells, cells.shape[dim] - 1, cells.shape[dim], axis=dim)
    return jnp.concatenate([shifted(tail, axis, 1), cells, shifted(head, axis, -1)], axis=dim)


def dot(left, right, left_dim, right_dim):
    return lax.dot_general(
        left, right, (((left_dim,), (right_dim,)), ((), ())), preferred_element_type=jnp.float32
    )


def butterfly_sum(x):
    stages = [("east", 1), ("tm", 1)]
    stages += [("north", 1 << i) for i in range(lax.axis_size("north").bit_length() - 1)]
    stages += [("east", 1 << i) for i in range(1, lax.axis_size("east").bit_length() - 1)]

    def swap(part, axis, bit):
        return lax.ppermute(part, axis, [(i, i ^ bit) for i in range(lax.axis_size(axis))])

    for axis, bit in stages:
        high = (lax.axis_index(axis) // bit) % 2
        half = x.shape[0] // 2
        keep = lax.dynamic_slice_in_dim(x, high * half, half, 0)
        send = lax.dynamic_slice_in_dim(x, (1 - high) * half, half, 0)
        x = keep + swap(send.astype(jnp.bfloat16), axis, bit).astype(jnp.float32)
    x = x.astype(jnp.bfloat16)
    for axis, bit in reversed(stages):
        high = (lax.axis_index(axis) // bit) % 2
        other = swap(x, axis, bit)
        x = jnp.concatenate(
            [jnp.where(high == 1, other, x), jnp.where(high == 1, x, other)], axis=0
        )
    return x.astype(jnp.float32)


def layer_kernel(
    own_slots,
    list_len,
    entry_ref,
    count_ref,
    table_ref,
    agent_ref,
    out_grad_ref,
    wq_ref,
    wkv_ref,
    wo_ref,
    attn_ref,
    part_ref,
    own_ref,
    query_term_ref,
    pair_term_ref,
    out_term_ref,
    kv_ref,
    acc_ref,
    kset_ref,
    vset_ref,
    bias_ref,
    score_ref,
    gprob_ref,
    prob_ref,
    gscore_ref,
    qbd_ref,
    gbd_ref,
):
    slots, rows, width = table_ref.shape
    blocks = agent_ref.shape[0]
    head_size = width // HEADS
    scale = 1.0 / math.sqrt(head_size)
    bf16 = jnp.bfloat16

    def project(i, c):
        at = pl.ds(i * 4, 4)
        kv = dot(table_ref[at].reshape(4 * rows, width), wkv_ref[...], 1, 0)
        kv_ref[at] = kv.astype(bf16).reshape(4, rows, 2 * width)
        acc_ref[at] = jnp.zeros((4, rows, 2 * width), jnp.float32)
        return c

    lax.fori_loop(0, slots // 4, project, 0)
    query_term_ref[...] = jnp.zeros_like(query_term_ref)
    pair_term_ref[...] = jnp.zeros_like(pair_term_ref)
    out_term_ref[...] = jnp.zeros_like(out_term_ref)
    lane = lax.broadcasted_iota(jnp.int32, (rows, width), 1)
    row = lax.broadcasted_iota(jnp.int32, (rows, width), 0)
    step = 3 * rows
    chunks = [pl.ds(i * step, step) for i in range(list_len // 3)]

    def diagonal(full):
        parts = [
            full[h * head_size : (h + 1) * head_size, h * rows : (h + 1) * rows]
            for h in range(HEADS)
        ]
        return jnp.concatenate(parts, axis=0).T

    def block(b, c):
        a = agent_ref[b]
        og = out_grad_ref[b]
        ok = row < count_ref[b]
        q = dot(a, wq_ref[...], 1, 0).astype(bf16).astype(jnp.float32) * scale
        g = jnp.where(ok, dot(og, wo_ref[...], 1, 1), 0.0)
        for h in range(HEADS):
            mine = (lane >= h * head_size) & (lane < (h + 1) * head_size)
            qbd_ref[pl.ds(h * rows, rows)] = jnp.where(mine, q, 0.0).astype(bf16)
            gbd_ref[pl.ds(h * rows, rows)] = jnp.where(mine, g, 0.0).astype(bf16)
        for e in range(list_len):
            entry = entry_ref[b * list_len + e]
            slot = jnp.maximum(entry, 0)
            at = pl.ds(e * rows, rows)
            kset_ref[at] = kv_ref[slot, :, :width]
            vset_ref[at] = kv_ref[slot, :, width:]
            mark = table_ref[slot, :, :128].astype(jnp.float32)
            gone = jnp.where(mark > EMPTY_ABOVE, NEG_FILL, 0.0)
            gone = jnp.where(entry < 0, NEG_FILL, gone)
            bias_ref[at] = jnp.broadcast_to(gone[:, :1], (rows, 128))
        top = jnp.full((1, HEADS * rows), 2 * NEG_FILL, jnp.float32)
        for at in chunks:
            s = dot(kset_ref[at], qbd_ref[...], 1, 1)
            s = s + jnp.concatenate([bias_ref[at]] * (HEADS * rows // 128), axis=1)
            score_ref[at] = s
            top = jnp.maximum(top, jnp.max(s, axis=0, keepdims=True))
            gprob_ref[at] = dot(vset_ref[at], gbd_ref[...], 1, 1)
        total = jnp.zeros_like(top)
        delta = jnp.zeros_like(top)
        for at in chunks:
            e = jnp.exp(score_ref[at] - top)
            score_ref[at] = e
            total = total + jnp.sum(e, axis=0, keepdims=True)
            delta = delta + jnp.sum(e * gprob_ref[at], axis=0, keepdims=True)
        inv = 1.0 / total
        delta = delta * inv
        for at in chunks:
            p = score_ref[at] * inv
            prob_ref[at] = p.astype(bf16)
            gscore_ref[at] = (p * (gprob_ref[at] - delta)).astype(bf16)
        for i, at in enumerate(chunks):
            gk = dot(gscore_ref[at], qbd_ref[...], 1, 0)
            gv = dot(prob_ref[at], gbd_ref[...], 1, 0)
            for j in range(3):
                slot = jnp.maximum(entry_ref[b * list_len + i * 3 + j], 0)
                acc_ref[slot, :, :width] += gk[j * rows : (j + 1) * rows]
                acc_ref[slot, :, width:] += gv[j * rows : (j + 1) * rows]
        att = diagonal(dot(vset_ref[...], prob_ref[...], 0, 0))
        gq = diagonal(dot(kset_ref[...], gscore_ref[...], 0, 0)) * scale
        att = jnp.where(ok, att, 0.0).astype(bf16)
        gq = gq.astype(bf16)
        attn_ref[b] = dot(att, wo_ref[...], 1, 0).astype(bf16)
        out_term_ref[...] += dot(att, og, 0, 0)
        query_term_ref[...] += dot(a, gq, 0, 0)
        own_ref[b] = dot(gq, wq_ref[...], 1, 1)
        return c

    lax.fori_loop(0, blocks, block, 0)

    def finish(i, c):
        at = pl.ds(i * 4, 4)
        pair = acc_ref[at].astype(bf16).reshape(4 * rows, 2 * width)
        pair_term_ref[...] += dot(table_ref[at].reshape(4 * rows, width), pair, 0, 0)
        part = dot(pair, wkv_ref[...], 1, 1)
        part_ref[at] = part.astype(bf16).reshape(4, rows, width)
        return c

    lax.fori_loop(0, slots // 4, finish, 0)
    for b, slot in enumerate(own_slots):
        pair = acc_ref[slot].astype(bf16)
        own_ref[b] += dot(pair, wkv_ref[...], 1, 1)


def per_device(
    agents,
    query_weight,
    key_weight,
    value_weight,
    out_weight,
    grad_output,
    same_lists,
    prev_lists,
    counts,
):
    _, east_blocks, north_blocks, rows, width = agents.shape
    own_blocks = east_blocks * north_blocks
    same_count = same_lists.shape[-1]
    list_len = same_count + prev_lists.shape[-1]
    span_east = east_blocks + 2
    span_north = north_blocks + 2
    rim = span_east * span_north
    row_index = jnp.arange(rows, dtype=jnp.int32)
    valid = row_index < counts[..., None]
    marked = jnp.where(valid[..., None], agents, jnp.asarray(MARK, agents.dtype))
    cells = jnp.concatenate([marked, shifted(marked, "tm", 1)], axis=0)
    cells = padded(padded(cells, "east", 1), "north", 2)
    table = cells.reshape(2 * rim, rows, width)
    grid_east = east_blocks * lax.axis_size("east")
    grid_north = north_blocks * lax.axis_size("north")
    first_east = lax.axis_index("east") * east_blocks
    first_north = lax.axis_index("north") * north_blocks

    def local_slot(ids, base):
        place = ids % (grid_east * grid_north)
        east_pos = place // grid_north - first_east + 1
        north_pos = place % grid_north - first_north + 1
        return jnp.where(ids >= 0, base + east_pos * span_north + north_pos, -1)

    entries = jnp.concatenate(
        [
            local_slot(same_lists.reshape(own_blocks, same_count), 0),
            local_slot(prev_lists.reshape(own_blocks, list_len - same_count), rim),
        ],
        axis=1,
    ).reshape(-1)
    own_slots = [
        (e + 1) * span_north + n + 1 for e in range(east_blocks) for n in range(north_blocks)
    ]
    keys = list_len * rows
    lanes = HEADS * rows
    f32, bf16 = jnp.float32, jnp.bfloat16
    vmem = pl.BlockSpec(memory_space=pltpu.VMEM)
    smem = pl.BlockSpec(memory_space=pltpu.SMEM)
    attn, part, own, query_term, pair_term, out_term = pl.pallas_call(
        lambda *refs: layer_kernel(own_slots, list_len, *refs),
        out_shape=(
            jax.ShapeDtypeStruct((own_blocks, rows, width), bf16),
            jax.ShapeDtypeStruct((2 * rim, rows, width), bf16),
            jax.ShapeDtypeStruct((own_blocks, rows, width), f32),
            jax.ShapeDtypeStruct((width, width), f32),
            jax.ShapeDtypeStruct((width, 2 * width), f32),
            jax.ShapeDtypeStruct((width, width), f32),
        ),
        in_specs=[smem, smem] + [vmem] * 6,
        out_specs=[vmem] * 6,
        scratch_shapes=[
            pltpu.VMEM((2 * rim, rows, 2 * width), bf16),
            pltpu.VMEM((2 * rim, rows, 2 * width), f32),
            pltpu.VMEM((keys, width), bf16),
            pltpu.VMEM((keys, width), bf16),
            pltpu.VMEM((keys, 128), f32),
            pltpu.VMEM((keys, lanes), f32),
            pltpu.VMEM((keys, lanes), f32),
            pltpu.VMEM((keys, lanes), bf16),
            pltpu.VMEM((keys, lanes), bf16),
            pltpu.VMEM((lanes, width), bf16),
            pltpu.VMEM((lanes, width), bf16),
        ],
        compiler_params=pltpu.CompilerParams(vmem_limit_bytes=56 * 1024 * 1024),
    )(
        entries,
        counts.reshape(-1),
        table,
        agents.reshape(own_blocks, rows, width),
        grad_output.reshape(own_blocks, rows, width),
        query_weight,
        jnp.concatenate([key_weight, value_weight], axis=1),
        out_weight,
    )
    part = part.reshape(2, span_east, span_north, rows, width)
    upper = shifted(part[:, :, -1], "north", 1)
    lower = shifted(part[:, :, 0], "north", -1)
    def edge(cells, at):
        col = cells[:, at].astype(f32)
        col = col.at[:, 0].add(upper[:, at].astype(f32))
        return col.at[:, -1].add(lower[:, at].astype(f32))

    inner = part[:, :, 1:-1]
    east_upper = shifted(edge(inner, span_east - 1).astype(bf16), "east", 1)
    east_lower = shifted(edge(inner, 0).astype(bf16), "east", -1)
    own_cells = own.reshape(1, east_blocks, north_blocks, rows, width)
    core = jnp.concatenate([own_cells, inner[1:, 1:-1].astype(f32)], axis=0)
    core = core.at[:, :, 0].add(upper[:, 1:-1].astype(f32))
    core = core.at[:, :, -1].add(lower[:, 1:-1].astype(f32))
    core = core.at[:, 0].add(east_upper.astype(f32))
    core = core.at[:, -1].add(east_lower.astype(f32))
    agent_grad = core[:1] + shifted(core[1:].astype(bf16), "tm", -1).astype(f32)
    agent_grad = agent_grad.astype(bf16)
    terms = [query_term, pair_term[:, :width], pair_term[:, width:], out_term]
    sums = butterfly_sum(jnp.concatenate(terms, axis=0)).reshape(4, width, width)
    total_rows = (
        lax.axis_size("tm")
        * lax.axis_size("east")
        * lax.axis_size("north")
        * own_blocks
        * rows
    )
    norm = 1.0 / math.sqrt(total_rows)
    return (
        attn.reshape(agents.shape),
        agent_grad,
        sums[0] * norm,
        sums[1] * norm,
        sums[2] * norm,
        sums[3] * norm,
    )


def solution(mesh):
    cells = P("tm", "east", "north", None, None)
    lists = P("tm", "east", "north", None)
    in_specs = (cells, P(), P(), P(), P(), cells, lists, lists, P("tm", "east", "north"))
    out_specs = (cells, cells, P(), P(), P(), P())
    return jax.shard_map(
        per_device, mesh=mesh, in_specs=in_specs, out_specs=out_specs, check_vma=False
    )
```
